256 devices in a mesh: star: 32 (over z, y), night: 8 (over x, core).
Axes of the slice: x: 4, y: 4, z: 8, core: 2. Of those that a mesh axis runs over, the one named last changes fastest.
Arguments:
- flux: bfloat16 [16, 262144], P('night', 'star'), may hold values from -6 to 6
- observed: int32 [16, 262144], P('night', 'star'), may hold values 0 or 1
- loadings: bfloat16 [262144, 64], P('star'), may hold values from -0.375 to 0.375
- channel: int32 [262144], P('star'), may hold values from 0 to 3
- decay: float32 [256], replicated, may hold values from 0.8 to 1
- mixing: float32 [256, 256], replicated, may hold values from -0.078125 to 0.078125
- process_precision: float32 [256], replicated, may hold values from 204.8 to 131072
Outputs:
- modes: float32 [16, 256], P('night')
- detrended: float32 [16, 262144], P('night', 'star')
The draws below stay inside these ranges and needn't reach their ends.
All inputs are finite; a program needn't handle non-finite values. No bound on the sum of `observed` on one device may be relied on, other than what follows from the above.
Results may differ from the reference program's by a relative error of at most 0.0003.
Values sent between devices are 32-bit elements; how exact they have to be, the bound alone decides.
No kernel may reach another device: no remote copies, remote signals or barrier semaphores. Data moves between devices by JAX's collectives and lax.ppermute only.
A program may use at most 64 MiB of HBM per device.

```python
import math
import jax
import jax.numpy as jnp
from jax import lax

K = 256
BLOCK = 64
GROUPS = 4
STARS = 262144
NIGHTS = 16


def channel_values(key):
    picks = jax.random.randint(jax.random.fold_in(key, 11), (STARS,), 0, GROUPS, dtype=jnp.int32)
    return picks.at[:GROUPS].set(jnp.arange(GROUPS, dtype=jnp.int32))


def loading_values(key):
    values = jax.random.normal(jax.random.fold_in(key, 12), (STARS, BLOCK), jnp.float32)
    return jnp.clip(values, -2.97, 2.97) / math.sqrt(BLOCK)


def draw_channel(key, part):
    return channel_values(key)


def draw_loadings(key, part):
    return loading_values(key).astype(jnp.bfloat16)


def draw_flux(key, part):
    channel = channel_values(key)
    loadings = loading_values(key).astype(jnp.bfloat16).astype(jnp.float32)
    night_axis = jnp.arange(NIGHTS, dtype=jnp.float32)[:, None]
    low_freq = math.log(math.pi / NIGHTS)
    freqs = jnp.exp(jax.random.uniform(jax.random.fold_in(key, 13), (K,), jnp.float32, low_freq, 0.0))
    phases = jax.random.uniform(jax.random.fold_in(key, 14), (K,), jnp.float32, -math.pi, math.pi)
    amps = jax.random.uniform(jax.random.fold_in(key, 15), (K,), jnp.float32, 0.5, 1.5)
    rough = 0.6 * jax.random.normal(jax.random.fold_in(key, 16), (NIGHTS, K), jnp.float32)
    noise = jax.random.normal(jax.random.fold_in(key, 18), (NIGHTS, STARS), jnp.float32)
    truth = amps[None, :] * jnp.sin(freqs[None, :] * night_axis + phases[None, :]) + rough
    trend = jnp.zeros((NIGHTS, STARS), jnp.float32)
    for group in range(GROUPS):
        part_trend = jnp.matmul(truth[:, group * BLOCK:(group + 1) * BLOCK], loadings.T, precision=lax.Precision.HIGHEST)
        trend = trend + jnp.where((channel == group)[None, :], part_trend, jnp.float32(0.0))
    return jnp.clip(trend + noise, -6.0, 6.0).astype(jnp.bfloat16)


def with_ends(drawn, key, low, top_value):
    extent = drawn.shape
    spot = [jax.random.randint(jax.random.fold_in(key, axis), (), 0, extent[axis]) for axis in range(len(extent))]
    drawn = drawn.at[tuple(spot)].set(low)
    longest = extent.index(max(extent))
    spot[longest] = (spot[longest] + 1) % extent[longest]
    return drawn.at[tuple(spot)].set(top_value)


def bell_draw(key, extent, width, most, held_as=jnp.bfloat16):
    entries = jax.random.normal(key, extent, jnp.float32) * width
    return jnp.minimum(jnp.maximum(entries, -most), most).astype(held_as)


def setup_inputs(seed: int = 0) -> dict:
    seeds = jax.random.split(jax.random.key(seed), 8)
    flux = draw_flux(jax.random.fold_in(seeds[7], 71), 0)
    observed = with_ends((jax.random.randint(seeds[1], (NIGHTS, STARS), 0, 4) < 3).astype(jnp.int32), jax.random.fold_in(seeds[1], 1), 0, 1)
    loadings = draw_loadings(jax.random.fold_in(seeds[7], 71), 0)
    channel = draw_channel(jax.random.fold_in(seeds[7], 71), 0)
    decay = jnp.clip(jax.random.uniform(seeds[4], (K,), jnp.float32, 0.8, 1.0), 0.8, 1.0)
    mixing = bell_draw(seeds[5], (K, K), (25 * K) ** -0.5, 0.078125, jnp.float32)
    process_precision = jnp.clip(jnp.exp(jax.random.uniform(seeds[6], (K,), jnp.float32, math.log(204.8), math.log(131072.0))), 204.8, 131072.0)
    return {"flux": flux, "observed": observed, "loadings": loadings, "channel": channel, "decay": decay, "mixing": mixing, "process_precision": process_precision}


highest = lax.Precision.HIGHEST

def product(left, right):
    return jnp.matmul(left, right, precision=highest)

def reference(flux, observed, loadings, channel, decay, mixing, process_precision):
    groups = K // BLOCK
    seen = observed.astype(jnp.bfloat16)
    weighted = flux * seen
    selectors = [(channel == group).astype(jnp.bfloat16) for group in range(groups)]

    def night_terms(inputs):
        seen_row, weighted_row = inputs
        gram = jnp.zeros((K, K), jnp.float32)
        pulls = []
        for group in range(groups):
            scaled = loadings * (seen_row * selectors[group])[:, None]
            block = jnp.dot(scaled.T.astype(jnp.float32), loadings.astype(jnp.float32), preferred_element_type=jnp.float32)
            gram = gram.at[group * BLOCK:(group + 1) * BLOCK, group * BLOCK:(group + 1) * BLOCK].set(block)
            pulls.append(jnp.dot((weighted_row * selectors[group]).astype(jnp.float32), loadings.astype(jnp.float32), preferred_element_type=jnp.float32))
        return (gram, jnp.concatenate(pulls))
    information, pull = lax.map(night_terms, (seen, weighted))
    transition = jnp.diag(decay) + mixing
    coupled = process_precision[:, None] * transition
    curvature = product(transition.T, coupled)
    base = jnp.diag(process_precision)
    firsts = jnp.arange(NIGHTS) == 0

    def forward(state, inputs):
        prev_end, prev_pull = state
        gram, pull_row, first = inputs
        solved = jnp.linalg.solve(prev_end + curvature, jnp.concatenate([coupled.T, prev_pull[:, None]], 1))
        end = base + gram - product(coupled, solved[:, :K])
        end_pull = pull_row + product(coupled, solved[:, K])
        end = jnp.where(first, base + gram, end)
        end_pull = jnp.where(first, pull_row, end_pull)
        return ((end, end_pull), (end, end_pull))
    start = (jnp.eye(K, dtype=jnp.float32), jnp.zeros((K,), jnp.float32))
    final_state, stacked = lax.scan(forward, start, (information, pull, firsts))
    ends, end_pulls = stacked
    last_mode = jnp.linalg.solve(ends[-1], end_pulls[-1])

    def backward(following, inputs):
        end, end_pull = inputs
        value = jnp.linalg.solve(end + curvature, end_pull + product(coupled.T, following))
        return (value, value)
    first_mode, earlier = lax.scan(backward, last_mode, (ends[:-1], end_pulls[:-1]), reverse=True)
    modes = jnp.concatenate([earlier, last_mode[None]], 0)
    trend = jnp.zeros((NIGHTS, flux.shape[1]), jnp.float32)
    wide_loadings = loadings.astype(jnp.float32)
    for group in range(groups):
        part = product(modes[:, group * BLOCK:(group + 1) * BLOCK], wide_loadings.T)
        trend = trend + jnp.where((channel == group)[None, :], part, jnp.float32(0.0))
    detrended = flux.astype(jnp.float32) - trend
    return (modes, detrended)
```

```python
import jax
import jax.numpy as jnp
from jax import lax
from jax.experimental import pallas as pl
from jax.experimental.pallas import tpu as pltpu
from jax.sharding import PartitionSpec as P

highest = lax.Precision.HIGHEST
f32 = jnp.float32
bf16 = jnp.bfloat16


def product(left, right):
    return jnp.matmul(left, right, precision=highest, preferred_element_type=f32)


def halves(value):
    high = value.astype(bf16)
    return high, (value - high.astype(f32)).astype(bf16)


def lhs_of(value):
    high, low = halves(value)
    return jnp.concatenate([high, high, low], 1)


def rhs_of(value):
    high, low = halves(value)
    return jnp.concatenate([high, low, high], 0)


def dot(left, right):
    return jnp.dot(left, right, preferred_element_type=f32)


def invert_blocks(cells):
    pairs, size, lanes = cells.shape
    groups = size // 8
    cells = cells.reshape(pairs, groups, 8, lanes)
    lane = lax.broadcasted_iota(jnp.int32, (8, lanes), 1)
    sub = lax.broadcasted_iota(jnp.int32, (8, lanes), 0)
    within = lane % size
    base = lane - within

    def eight(turn, cells):
        rows = [[cells[p, g] for g in range(groups)] for p in range(pairs)]
        for r in range(8):
            spot = turn * 8 + r
            pick = base + spot
            hit = within == spot
            for p in range(pairs):
                cols = [jnp.take_along_axis(rows[p][g], pick, axis=1) for g in range(groups)]
                inverse = 1.0 / jnp.broadcast_to(cols[0][r : r + 1], (8, lanes))
                lead = jnp.broadcast_to(rows[p][0][r : r + 1], (8, lanes))
                lead = jnp.where(hit, inverse, lead * inverse)
                fresh = [jnp.where(hit, 0.0, rows[p][g]) - cols[g] * lead for g in range(groups)]
                fresh[0] = jnp.where(sub == r, lead, fresh[0])
                rows[p] = fresh
        return jnp.stack([jnp.stack(rows[p][1:] + rows[p][:1], 0) for p in range(pairs)], 0)

    cells = lax.fori_loop(0, groups, eight, cells)
    return cells.reshape(pairs, size, lanes)


def make_solver(nights, width, block):
    groups = width // block
    levels = nights.bit_length() - 1
    offsets = [0]
    for level in range(1, levels):
        offsets.append(offsets[-1] + (0 if level == 1 else nights >> (level - 1)))
    slots = sum(nights >> level for level in range(1, levels + 1))

    def body(info, pull, cross, cross_t, curve, gscale, scale, modes, diag, saved, chain, chain_t, blocks, vb_ref, b_ref, r_ref, q_ref):
        row = lax.broadcasted_iota(jnp.int32, (width, width), 0)
        col = lax.broadcasted_iota(jnp.int32, (width, width), 1)
        eye = jnp.where(row == col, 1.0, 0.0).astype(f32)
        lanes = lax.broadcasted_iota(jnp.int32, (width, width), 1)
        same = (row // block) == (col // block)

        def build(t, _):
            part = info[t] * gscale[...]
            wide = jnp.concatenate([part] * groups, 1)
            whole = jnp.where(same, wide, 0.0) + eye
            whole = whole + jnp.where(t < nights - 1, curve[...], 0.0)
            diag[t] = whole
            saved[t] = whole
            return 0

        lax.fori_loop(0, nights, build, 0)

        def invert(node_of, count):
            pairs = max(count // 2, 1)
            for kb in range(groups):
                lo = kb * block
                packed = []
                for p in range(pairs):
                    first = diag[node_of(2 * p), lo : lo + block, lo : lo + block]
                    second = diag[node_of(2 * p + (1 if count > 1 else 0)), lo : lo + block, lo : lo + block]
                    packed.append(jnp.concatenate([first, second], 1))
                done = invert_blocks(jnp.stack(packed, 0))
                for p in range(pairs):
                    blocks[p] = done[p]

                def sweep(p, _):
                    for side in range(2 if count > 1 else 1):
                        node = node_of(2 * p + side)
                        pivot = blocks[p][:, side * block : (side + 1) * block]
                        lead = diag[node, lo : lo + block, :]
                        lead = dot(lhs_of(pivot), rhs_of(lead))
                        tall = [pivot if g == kb else jnp.zeros((block, block), f32) for g in range(groups)]
                        mine = (lax.broadcasted_iota(jnp.int32, (block, width), 1) // block) == kb
                        lead = jnp.where(mine, jnp.concatenate(tall, 1), lead)
                        others = [g for g in range(groups) if g != kb]
                        wing = jnp.concatenate([diag[node, g * block : (g + 1) * block, lo : lo + block] for g in others], 0)
                        change = dot(lhs_of(wing), rhs_of(lead))
                        for n, g in enumerate(others):
                            old = diag[node, g * block : (g + 1) * block, :]
                            diag[node, g * block : (g + 1) * block, :] = jnp.where(mine, 0.0, old) - change[n * block : (n + 1) * block]
                        diag[node, lo : lo + block, :] = lead
                    return 0

                if pairs == 1:
                    sweep(0, 0)
                else:
                    lax.fori_loop(0, pairs, sweep, 0)

        def node_at(level):
            return lambda place: (place + 1) * (1 << level) - 1

        def el(level, m):
            return cross[...] if level == 0 else chain[offsets[level] + 2 * m]

        def el_t(level, m):
            return cross_t[...] if level == 0 else chain_t[offsets[level] + 2 * m]

        def er(level, m):
            return cross[...] if level == 0 else chain[offsets[level] + 2 * m + 1]

        def er_t(level, m):
            return cross_t[...] if level == 0 else chain_t[offsets[level] + 2 * m + 1]

        def q_slot(level, m):
            return sum(nights >> (j + 1) for j in range(level)) + m

        for level in range(levels):
            at = node_at(level)
            count = nights >> (level + 1)
            invert(lambda m: at(2 * m), count)
            mid = rhs_of(diag[at(0)])
            flow = dot(lhs_of(er(level, 0)), mid)
            q_ref[q_slot(level, 0), width:] = flow
            diag[at(1)] = diag[at(1)] - dot(lhs_of(flow), rhs_of(er_t(level, 0)))

            def eliminate(m, _):
                middle = rhs_of(diag[at(2 * m)])
                flow = dot(jnp.concatenate([lhs_of(el_t(level, m)), lhs_of(er(level, m))], 0), middle)
                q_ref[q_slot(level, m)] = flow
                spread = dot(lhs_of(flow), jnp.concatenate([rhs_of(el(level, m)), rhs_of(er_t(level, m))], 1))
                diag[at(2 * m - 1)] = diag[at(2 * m - 1)] - spread[:width, :width]
                diag[at(2 * m + 1)] = diag[at(2 * m + 1)] - spread[width:, width:]
                if level + 1 < levels:
                    chain[offsets[level + 1] + m] = spread[width:, :width]
                    chain_t[offsets[level + 1] + m] = spread[:width, width:]
                return 0

            if count == 2:
                eliminate(1, 0)
            elif count > 2:
                lax.fori_loop(1, count, eliminate, 0)
        invert(lambda m: nights - 1, 1)

        def apply(matrix, column):
            return jnp.sum(matrix * column, 0, keepdims=True)

        def backsolve():
            for level in range(levels + 1):
                at = node_at(level)
                count = max(nights >> (level + 1), 1)
                cols = b_ref[...].T
                for m in range(count):
                    node = at(2 * m)
                    vb_ref[node : node + 1] = apply(diag[node], cols[:, node : node + 1])
                if level == levels:
                    break
                cols = vb_ref[...].T
                for m in range(count):
                    node = at(2 * m)
                    column = cols[:, node : node + 1]
                    if m:
                        left = at(2 * m - 1)
                        b_ref[left : left + 1] = b_ref[left : left + 1] + apply(el(level, m), column)
                    right = at(2 * m + 1)
                    b_ref[right : right + 1] = b_ref[right : right + 1] + apply(er_t(level, m), column)
            for level in range(levels - 1, -1, -1):
                at = node_at(level)
                cols = vb_ref[...].T
                for m in range(nights >> (level + 1)):
                    node, right = at(2 * m), at(2 * m + 1)
                    value = vb_ref[node : node + 1] + apply(q_ref[q_slot(level, m), width:], cols[:, right : right + 1])
                    if m:
                        left = at(2 * m - 1)
                        value = value + apply(q_ref[q_slot(level, m), :width], cols[:, left : left + 1])
                    vb_ref[node : node + 1] = value

        start = pull[...] * scale[...]
        b_ref[...] = start
        vb_ref[...] = jnp.zeros_like(vb_ref)
        backsolve()
        guess = vb_ref[...]
        cols = guess.T
        for t in range(nights):
            r_ref[t : t + 1] = apply(saved[t], cols[:, t : t + 1])
        ahead = product(guess, cross_t[...])
        behind = product(guess, cross[...])
        zero = jnp.zeros((1, width), f32)
        rest = start - r_ref[...]
        rest = rest + jnp.concatenate([zero, ahead[:-1]], 0) + jnp.concatenate([behind[1:], zero], 0)
        b_ref[...] = rest
        backsolve()
        modes[...] = (guess + vb_ref[...]) * scale[...]

    def solve(info, pull, cross, cross_t, curve, gscale, scale):
        vm = pltpu.VMEM
        count = sum(nights >> (j + 1) for j in range(levels))
        return pl.pallas_call(
            body,
            out_shape=jax.ShapeDtypeStruct((nights, width), f32),
            scratch_shapes=[
                vm((nights, width, width), f32),
                vm((nights, width, width), f32),
                vm((max(slots - nights // 2, 1) + 8, width, width), f32),
                vm((max(slots - nights // 2, 1) + 8, width, width), f32),
                vm((max(nights // 4, 1), block, 2 * block), f32),
                vm((nights, width), f32),
                vm((nights, width), f32),
                vm((nights, width), f32),
                vm((count, 2 * width, width), f32),
            ],
            compiler_params=pltpu.CompilerParams(vmem_limit_bytes=56 << 20),
        )(info, pull, cross, cross_t, curve, gscale, scale)

    return solve


def exchange(value, axis, mask):
    count = lax.axis_size(axis)
    return lax.ppermute(value, axis, [(i, i ^ mask) for i in range(count)])


def per_device(flux, observed, loadings, channel, decay, mixing, process_precision):
    nights, stars = flux.shape
    block = loadings.shape[1]
    width = mixing.shape[0]
    groups = width // block
    seen = observed.astype(bf16)
    member = channel[None, :] == jnp.arange(groups)[:, None]
    picks = (seen[:, None, :] * member[None].astype(bf16)).reshape(nights * groups, stars)
    flat = loadings.T
    masked = (picks[:, None, :] * flat[None]).reshape(nights * groups * block, stars)
    grams = jnp.dot(masked, loadings, preferred_element_type=f32).reshape(nights, width, block)
    pulls = jnp.dot((flux[:, None, :] * picks.reshape(nights, groups, stars)).reshape(nights * groups, stars), loadings, preferred_element_type=f32)
    pulls = pulls.reshape(nights, width)
    packed = jnp.concatenate([grams.reshape(nights, width * block // 128, 128), pulls.reshape(nights, width // 128, 128)], 1)
    mask = 1
    while mask < lax.axis_size("star"):
        packed = packed + exchange(packed, "star", mask)
        mask *= 2
    rank = lax.axis_index("night")
    mask = 1
    whole = packed[None]
    while mask < lax.axis_size("night"):
        other = exchange(whole, "night", mask)
        low = (rank & mask) == 0
        whole = jnp.where(low, jnp.concatenate([whole, other], 0), jnp.concatenate([other, whole], 0))
        mask *= 2
    total = lax.axis_size("night") * nights
    whole = whole.reshape(total, -1, 128)
    info = whole[:, : width * block // 128].reshape(total, width, block)
    pull = whole[:, width * block // 128 :].reshape(total, width)

    root = jnp.sqrt(process_precision)
    down = 1.0 / root
    transition = jnp.diag(decay) + mixing
    cross = root[:, None] * transition * down[None, :]
    cross_t = cross.T
    curve = product(cross_t, cross)
    gscale = (down.reshape(groups, block, 1) * down.reshape(groups, 1, block)).reshape(width, block)
    solve = make_solver(total, width, block)
    all_modes = solve(info, pull, cross, cross_t, curve, gscale, down[None, :])
    modes = lax.dynamic_slice(all_modes, (rank * nights, 0), (nights, width))

    parts = []
    rest = modes.reshape(nights * groups, block)
    for _ in range(3):
        piece = lax.reduce_precision(rest, 8, 7)
        parts.append(piece.astype(bf16))
        rest = rest - piece
    fits = jnp.dot(jnp.concatenate(parts, 0), flat, preferred_element_type=f32).reshape(3, nights, groups, stars)
    fits = fits[0] + (fits[1] + fits[2])
    trend = jnp.zeros((nights, stars), f32)
    for group in range(groups):
        trend = jnp.where(member[group][None], fits[:, group], trend)
    return (modes, flux.astype(f32) - trend)


def solution(mesh):
    return jax.shard_map(
        per_device,
        mesh=mesh,
        in_specs=(P("night", "star"), P("night", "star"), P("star", None), P("star"), P(), P(), P()),
        out_specs=(P("night", None), P("night", "star")),
        check_vma=False,
    )
```

```python
import jax
import jax.numpy as jnp
from jax import lax
from jax.experimental import pallas as pl
from jax.experimental.pallas import tpu as pltpu
from jax.sharding import PartitionSpec as P

highest = lax.Precision.HIGHEST
f32 = jnp.float32
bf16 = jnp.bfloat16


def product(left, right):
    return jnp.matmul(left, right, precision=highest, preferred_element_type=f32)


def halves(value):
    high = value.astype(bf16)
    return high, (value - high.astype(f32)).astype(bf16)


def lhs_of(value):
    high, low = halves(value)
    return jnp.concatenate([high, high, low], 1)


def rhs_of(value):
    high, low = halves(value)
    return jnp.concatenate([high, low, high], 0)


def dot(left, right):
    return jnp.dot(left, right, preferred_element_type=f32)


def invert_blocks(cells):
    pairs, size, lanes = cells.shape
    groups = size // 8
    cells = cells.reshape(pairs, groups, 8, lanes)
    lane = lax.broadcasted_iota(jnp.int32, (8, lanes), 1)
    sub = lax.broadcasted_iota(jnp.int32, (8, lanes), 0)
    within = lane % size
    base = lane - within

    def eight(turn, cells):
        first = turn * 8
        picks = [base + (first + r) for r in range(8)]
        hits = [within == first + r for r in range(8)]
        inside = (within // 8) == turn
        leads = [cells[p, 0] for p in range(pairs)]
        panels = [[jnp.take_along_axis(leads[p], picks[r], axis=1) for r in range(8)] for p in range(pairs)]
        for r in range(8):
            for p in range(pairs):
                panel = panels[p]
                inverse = 1.0 / jnp.broadcast_to(panel[r][r : r + 1], (8, lanes))
                for j in range(r + 1, 8):
                    step = jnp.broadcast_to(panel[j][r : r + 1], (8, lanes)) * inverse
                    panel[j] = jnp.where(sub == r, step, panel[j] - panel[r] * step)
                lead = jnp.broadcast_to(leads[p][r : r + 1], (8, lanes)) * inverse
                lead = jnp.where(hits[r], inverse, lead)
                fresh = jnp.where(hits[r], 0.0, leads[p]) - panel[r] * lead
                leads[p] = jnp.where(sub == r, lead, fresh)
        done = []
        for p in range(pairs):
            spread = [jnp.broadcast_to(leads[p][r : r + 1], (8, lanes)) for r in range(8)]
            rest = []
            for g in range(1, groups):
                old = cells[p, g]
                cols = [jnp.take_along_axis(old, picks[r], axis=1) * spread[r] for r in range(8)]
                while len(cols) > 1:
                    cols = [cols[n] + cols[n + 1] for n in range(0, len(cols), 2)]
                rest.append(jnp.where(inside, 0.0, old) - cols[0])
            done.append(jnp.stack(rest + [leads[p]], 0))
        return jnp.stack(done, 0)

    cells = lax.fori_loop(0, groups, eight, cells)
    return cells.reshape(pairs, size, lanes)


def make_solver(nights, width, block):
    groups = width // block
    levels = nights.bit_length() - 1
    offsets = [0]
    for level in range(1, levels):
        offsets.append(offsets[-1] + (0 if level == 1 else nights >> (level - 1)))
    slots = sum(nights >> level for level in range(1, levels + 1))

    def body(info, pull, cross, cross_t, curve, gscale, scale, modes, diag, saved, chain, chain_t, blocks, vb_ref, b_ref, r_ref, q_ref):
        row = lax.broadcasted_iota(jnp.int32, (width, width), 0)
        col = lax.broadcasted_iota(jnp.int32, (width, width), 1)
        eye = jnp.where(row == col, 1.0, 0.0).astype(f32)
        lanes = lax.broadcasted_iota(jnp.int32, (width, width), 1)
        same = (row // block) == (col // block)

        def build(t, _):
            part = info[t] * gscale[...]
            wide = jnp.concatenate([part] * groups, 1)
            whole = jnp.where(same, wide, 0.0) + eye
            whole = whole + jnp.where(t < nights - 1, curve[...], 0.0)
            diag[t] = whole
            saved[t] = whole
            return 0

        lax.fori_loop(0, nights, build, 0)

        def invert(node_of, count):
            pairs = max(count // 2, 1)
            for kb in range(groups):
                lo = kb * block
                packed = []
                for p in range(pairs):
                    first = diag[node_of(2 * p), lo : lo + block, lo : lo + block]
                    second = diag[node_of(2 * p + (1 if count > 1 else 0)), lo : lo + block, lo : lo + block]
                    packed.append(jnp.concatenate([first, second], 1))
                done = invert_blocks(jnp.stack(packed, 0))
                for p in range(pairs):
                    blocks[p] = done[p]

                def sweep(p, _):
                    for side in range(2 if count > 1 else 1):
                        node = node_of(2 * p + side)
                        pivot = blocks[p][:, side * block : (side + 1) * block]
                        lead = diag[node, lo : lo + block, :]
                        lead = dot(lhs_of(pivot), rhs_of(lead))
                        tall = [pivot if g == kb else jnp.zeros((block, block), f32) for g in range(groups)]
                        mine = (lax.broadcasted_iota(jnp.int32, (block, width), 1) // block) == kb
                        lead = jnp.where(mine, jnp.concatenate(tall, 1), lead)
                        others = [g for g in range(groups) if g != kb]
                        wing = jnp.concatenate([diag[node, g * block : (g + 1) * block, lo : lo + block] for g in others], 0)
                        change = dot(lhs_of(wing), rhs_of(lead))
                        for n, g in enumerate(others):
                            old = diag[node, g * block : (g + 1) * block, :]
                            diag[node, g * block : (g + 1) * block, :] = jnp.where(mine, 0.0, old) - change[n * block : (n + 1) * block]
                        diag[node, lo : lo + block, :] = lead
                    return 0

                if pairs == 1:
                    sweep(0, 0)
                else:
                    lax.fori_loop(0, pairs, sweep, 0)

        def node_at(level):
            return lambda place: (place + 1) * (1 << level) - 1

        def el(level, m):
            return cross[...] if level == 0 else chain[offsets[level] + 2 * m]

        def el_t(level, m):
            return cross_t[...] if level == 0 else chain_t[offsets[level] + 2 * m]

        def er(level, m):
            return cross[...] if level == 0 else chain[offsets[level] + 2 * m + 1]

        def er_t(level, m):
            return cross_t[...] if level == 0 else chain_t[offsets[level] + 2 * m + 1]

        def q_slot(level, m):
            return sum(nights >> (j + 1) for j in range(level)) + m

        for level in range(levels):
            at = node_at(level)
            count = nights >> (level + 1)
            invert(lambda m: at(2 * m), count)
            mid = rhs_of(diag[at(0)])
            flow = dot(lhs_of(er(level, 0)), mid)
            q_ref[q_slot(level, 0), width:] = flow
            diag[at(1)] = diag[at(1)] - dot(lhs_of(flow), rhs_of(er_t(level, 0)))

            def eliminate(m, _):
                middle = rhs_of(diag[at(2 * m)])
                flow = dot(jnp.concatenate([lhs_of(el_t(level, m)), lhs_of(er(level, m))], 0), middle)
                q_ref[q_slot(level, m)] = flow
                spread = dot(lhs_of(flow), jnp.concatenate([rhs_of(el(level, m)), rhs_of(er_t(level, m))], 1))
                diag[at(2 * m - 1)] = diag[at(2 * m - 1)] - spread[:width, :width]
                diag[at(2 * m + 1)] = diag[at(2 * m + 1)] - spread[width:, width:]
                if level + 1 < levels:
                    chain[offsets[level + 1] + m] = spread[width:, :width]
                    chain_t[offsets[level + 1] + m] = spread[:width, width:]
                return 0

            if count == 2:
                eliminate(1, 0)
            elif count > 2:
                lax.fori_loop(1, count, eliminate, 0)
        invert(lambda m: nights - 1, 1)

        def apply(matrix, column):
            return jnp.sum(matrix * column, 0, keepdims=True)

        def backsolve():
            for level in range(levels + 1):
                at = node_at(level)
                count = max(nights >> (level + 1), 1)
                cols = b_ref[...].T
                for m in range(count):
                    node = at(2 * m)
                    vb_ref[node : node + 1] = apply(diag[node], cols[:, node : node + 1])
                if level == levels:
                    break
                cols = vb_ref[...].T
                for m in range(count):
                    node = at(2 * m)
                    column = cols[:, node : node + 1]
                    if m:
                        left = at(2 * m - 1)
                        b_ref[left : left + 1] = b_ref[left : left + 1] + apply(el(level, m), column)
                    right = at(2 * m + 1)
                    b_ref[right : right + 1] = b_ref[right : right + 1] + apply(er_t(level, m), column)
            for level in range(levels - 1, -1, -1):
                at = node_at(level)
                cols = vb_ref[...].T
                for m in range(nights >> (level + 1)):
                    node, right = at(2 * m), at(2 * m + 1)
                    value = vb_ref[node : node + 1] + apply(q_ref[q_slot(level, m), width:], cols[:, right : right + 1])
                    if m:
                        left = at(2 * m - 1)
                        value = value + apply(q_ref[q_slot(level, m), :width], cols[:, left : left + 1])
                    vb_ref[node : node + 1] = value

        start = pull[...] * scale[...]
        b_ref[...] = start
        vb_ref[...] = jnp.zeros_like(vb_ref)
        backsolve()
        guess = vb_ref[...]
        cols = guess.T
        for t in range(nights):
            r_ref[t : t + 1] = apply(saved[t], cols[:, t : t + 1])
        ahead = product(guess, cross_t[...])
        behind = product(guess, cross[...])
        zero = jnp.zeros((1, width), f32)
        rest = start - r_ref[...]
        rest = rest + jnp.concatenate([zero, ahead[:-1]], 0) + jnp.concatenate([behind[1:], zero], 0)
        b_ref[...] = rest
        backsolve()
        modes[...] = (guess + vb_ref[...]) * scale[...]

    def solve(info, pull, cross, cross_t, curve, gscale, scale):
        vm = pltpu.VMEM
        count = sum(nights >> (j + 1) for j in range(levels))
        return pl.pallas_call(
            body,
            out_shape=jax.ShapeDtypeStruct((nights, width), f32),
            scratch_shapes=[
                vm((nights, width, width), f32),
                vm((nights, width, width), f32),
                vm((max(slots - nights // 2, 1) + 8, width, width), f32),
                vm((max(slots - nights // 2, 1) + 8, width, width), f32),
                vm((max(nights // 4, 1), block, 2 * block), f32),
                vm((nights, width), f32),
                vm((nights, width), f32),
                vm((nights, width), f32),
                vm((count, 2 * width, width), f32),
            ],
            compiler_params=pltpu.CompilerParams(vmem_limit_bytes=56 << 20),
        )(info, pull, cross, cross_t, curve, gscale, scale)

    return solve


def exchange(value, axis, mask):
    count = lax.axis_size(axis)
    return lax.ppermute(value, axis, [(i, i ^ mask) for i in range(count)])


def per_device(flux, observed, loadings, channel, decay, mixing, process_precision):
    nights, stars = flux.shape
    block = loadings.shape[1]
    width = mixing.shape[0]
    groups = width // block
    seen = observed.astype(bf16)
    member = channel[None, :] == jnp.arange(groups)[:, None]
    picks = (seen[:, None, :] * member[None].astype(bf16)).reshape(nights * groups, stars)
    flat = loadings.T
    masked = (picks[:, None, :] * flat[None]).reshape(nights * groups * block, stars)
    grams = jnp.dot(masked, loadings, preferred_element_type=f32).reshape(nights, width, block)
    pulls = jnp.dot((flux[:, None, :] * picks.reshape(nights, groups, stars)).reshape(nights * groups, stars), loadings, preferred_element_type=f32)
    pulls = pulls.reshape(nights, width)
    packed = jnp.concatenate([grams.reshape(nights, width * block // 128, 128), pulls.reshape(nights, width // 128, 128)], 1)
    mask = 1
    while mask < lax.axis_size("star"):
        packed = packed + exchange(packed, "star", mask)
        mask *= 2
    rank = lax.axis_index("night")
    mask = 1
    whole = packed[None]
    while mask < lax.axis_size("night"):
        other = exchange(whole, "night", mask)
        low = (rank & mask) == 0
        whole = jnp.where(low, jnp.concatenate([whole, other], 0), jnp.concatenate([other, whole], 0))
        mask *= 2
    total = lax.axis_size("night") * nights
    whole = whole.reshape(total, -1, 128)
    info = whole[:, : width * block // 128].reshape(total, width, block)
    pull = whole[:, width * block // 128 :].reshape(total, width)

    root = jnp.sqrt(process_precision)
    down = 1.0 / root
    transition = jnp.diag(decay) + mixing
    cross = root[:, None] * transition * down[None, :]
    cross_t = cross.T
    curve = product(cross_t, cross)
    gscale = (down.reshape(groups, block, 1) * down.reshape(groups, 1, block)).reshape(width, block)
    solve = make_solver(total, width, block)
    all_modes = solve(info, pull, cross, cross_t, curve, gscale, down[None, :])
    modes = lax.dynamic_slice(all_modes, (rank * nights, 0), (nights, width))

    parts = []
    rest = modes.reshape(nights * groups, block)
    for _ in range(3):
        piece = lax.reduce_precision(rest, 8, 7)
        parts.append(piece.astype(bf16))
        rest = rest - piece
    fits = jnp.dot(jnp.concatenate(parts, 0), flat, preferred_element_type=f32).reshape(3, nights, groups, stars)
    fits = fits[0] + (fits[1] + fits[2])
    trend = jnp.zeros((nights, stars), f32)
    for group in range(groups):
        trend = jnp.where(member[group][None], fits[:, group], trend)
    return (modes, flux.astype(f32) - trend)


def solution(mesh):
    return jax.shard_map(
        per_device,
        mesh=mesh,
        in_specs=(P("night", "star"), P("night", "star"), P("star", None), P("star"), P(), P(), P()),
        out_specs=(P("night", None), P("night", "star")),
        check_vma=False,
    )
```

```python
import jax
import jax.numpy as jnp
from jax import lax
from jax.experimental import pallas as pl
from jax.experimental.pallas import tpu as pltpu
from jax.sharding import PartitionSpec as P

highest = lax.Precision.HIGHEST
f32 = jnp.float32
bf16 = jnp.bfloat16


def product(left, right):
    return jnp.matmul(left, right, precision=highest, preferred_element_type=f32)


def halves(value):
    high = value.astype(bf16)
    return high, (value - high.astype(f32)).astype(bf16)


def lhs_of(value):
    high, low = halves(value)
    return jnp.concatenate([high, high, low], 1)


def rhs_of(value):
    high, low = halves(value)
    return jnp.concatenate([high, low, high], 0)


def dot(left, right):
    return jnp.dot(left, right, preferred_element_type=f32)


def invert_blocks(cells):
    pairs, size, lanes = cells.shape
    groups = size // 8
    cells = cells.reshape(pairs, groups, 8, lanes)
    lane = lax.broadcasted_iota(jnp.int32, (8, lanes), 1)
    sub = lax.broadcasted_iota(jnp.int32, (8, lanes), 0)
    within = lane % size
    base = lane - within

    def eight(turn, cells):
        first = turn * 8
        picks = [base + (first + r) for r in range(8)]
        hits = [within == first + r for r in range(8)]
        inside = (within // 8) == turn
        leads = [cells[p, 0] for p in range(pairs)]
        panels = [[jnp.take_along_axis(leads[p], picks[r], axis=1) for r in range(8)] for p in range(pairs)]
        for r in range(8):
            for p in range(pairs):
                panel = panels[p]
                inverse = 1.0 / jnp.broadcast_to(panel[r][r : r + 1], (8, lanes))
                for j in range(r + 1, 8):
                    step = jnp.broadcast_to(panel[j][r : r + 1], (8, lanes)) * inverse
                    panel[j] = jnp.where(sub == r, step, panel[j] - panel[r] * step)
                lead = jnp.broadcast_to(leads[p][r : r + 1], (8, lanes)) * inverse
                lead = jnp.where(hits[r], inverse, lead)
                fresh = jnp.where(hits[r], 0.0, leads[p]) - panel[r] * lead
                leads[p] = jnp.where(sub == r, lead, fresh)
        done = []
        for p in range(pairs):
            spread = [jnp.broadcast_to(leads[p][r : r + 1], (8, lanes)) for r in range(8)]
            rest = []
            for g in range(1, groups):
                old = cells[p, g]
                cols = [jnp.take_along_axis(old, picks[r], axis=1) * spread[r] for r in range(8)]
                while len(cols) > 1:
                    cols = [cols[n] + cols[n + 1] for n in range(0, len(cols), 2)]
                rest.append(jnp.where(inside, 0.0, old) - cols[0])
            done.append(jnp.stack(rest + [leads[p]], 0))
        return jnp.stack(done, 0)

    cells = lax.fori_loop(0, groups, eight, cells)
    return cells.reshape(pairs, size, lanes)


def make_solver(nights, width, block):
    groups = width // block
    levels = nights.bit_length() - 1
    offsets = [0]
    for level in range(1, levels):
        offsets.append(offsets[-1] + (0 if level == 1 else nights >> (level - 1)))
    slots = sum(nights >> level for level in range(1, levels + 1))

    def body(info, pull, cross, cross_t, curve, gscale, scale, modes, diag, saved, chain, chain_t, blocks, vb_ref, b_ref, r_ref, q_ref):
        row = lax.broadcasted_iota(jnp.int32, (width, width), 0)
        col = lax.broadcasted_iota(jnp.int32, (width, width), 1)
        eye = jnp.where(row == col, 1.0, 0.0).astype(f32)
        lanes = lax.broadcasted_iota(jnp.int32, (width, width), 1)
        same = (row // block) == (col // block)

        def build(t, _):
            part = info[t] * gscale[...]
            wide = jnp.concatenate([part] * groups, 1)
            whole = jnp.where(same, wide, 0.0) + eye
            whole = whole + jnp.where(t < nights - 1, curve[...], 0.0)
            diag[t] = whole
            saved[t] = whole
            return 0

        lax.fori_loop(0, nights, build, 0)

        def invert(node_of, count):
            pairs = max(count // 2, 1)
            for kb in range(groups):
                lo = kb * block
                packed = []
                for p in range(pairs):
                    first = diag[node_of(2 * p), lo : lo + block, lo : lo + block]
                    second = diag[node_of(2 * p + (1 if count > 1 else 0)), lo : lo + block, lo : lo + block]
                    packed.append(jnp.concatenate([first, second], 1))
                done = invert_blocks(jnp.stack(packed, 0))
                for p in range(pairs):
                    blocks[p] = done[p]

                def sweep(p, _):
                    for side in range(2 if count > 1 else 1):
                        node = node_of(2 * p + side)
                        pivot = blocks[p][:, side * block : (side + 1) * block]
                        lead = diag[node, lo : lo + block, :]
                        lead = dot(lhs_of(pivot), rhs_of(lead))
                        tall = [pivot if g == kb else jnp.zeros((block, block), f32) for g in range(groups)]
                        mine = (lax.broadcasted_iota(jnp.int32, (block, width), 1) // block) == kb
                        lead = jnp.where(mine, jnp.concatenate(tall, 1), lead)
                        others = [g for g in range(groups) if g != kb]
                        wing = jnp.concatenate([diag[node, g * block : (g + 1) * block, lo : lo + block] for g in others], 0)
                        change = dot(lhs_of(wing), rhs_of(lead))
                        for n, g in enumerate(others):
                            old = diag[node, g * block : (g + 1) * block, :]
                            diag[node, g * block : (g + 1) * block, :] = jnp.where(mine, 0.0, old) - change[n * block : (n + 1) * block]
                        diag[node, lo : lo + block, :] = lead
                    return 0

                if pairs == 1:
                    sweep(0, 0)
                else:
                    lax.fori_loop(0, pairs, sweep, 0)

        def node_at(level):
            return lambda place: (place + 1) * (1 << level) - 1

        def el(level, m):
            return cross[...] if level == 0 else chain[offsets[level] + 2 * m]

        def el_t(level, m):
            return cross_t[...] if level == 0 else chain_t[offsets[level] + 2 * m]

        def er(level, m):
            return cross[...] if level == 0 else chain[offsets[level] + 2 * m + 1]

        def er_t(level, m):
            return cross_t[...] if level == 0 else chain_t[offsets[level] + 2 * m + 1]

        def q_slot(level, m):
            return sum(nights >> (j + 1) for j in range(level)) + m

        for level in range(levels):
            at = node_at(level)
            count = nights >> (level + 1)
            invert(lambda m: at(2 * m), count)
            mid = rhs_of(diag[at(0)])
            flow = dot(lhs_of(er(level, 0)), mid)
            q_ref[q_slot(level, 0), width:] = flow
            diag[at(1)] = diag[at(1)] - dot(lhs_of(flow), rhs_of(er_t(level, 0)))

            def eliminate(m, _):
                middle = rhs_of(diag[at(2 * m)])
                flow = dot(jnp.concatenate([lhs_of(el_t(level, m)), lhs_of(er(level, m))], 0), middle)
                q_ref[q_slot(level, m)] = flow
                spread = dot(lhs_of(flow), jnp.concatenate([rhs_of(el(level, m)), rhs_of(er_t(level, m))], 1))
                diag[at(2 * m - 1)] = diag[at(2 * m - 1)] - spread[:width, :width]
                diag[at(2 * m + 1)] = diag[at(2 * m + 1)] - spread[width:, width:]
                if level + 1 < levels:
                    chain[offsets[level + 1] + m] = spread[width:, :width]
                    chain_t[offsets[level + 1] + m] = spread[:width, width:]
                return 0

            if count == 2:
                eliminate(1, 0)
            elif count > 2:
                lax.fori_loop(1, count, eliminate, 0)
        invert(lambda m: nights - 1, 1)

        def apply(matrix, column):
            return jnp.sum(matrix * column, 0, keepdims=True)

        def backsolve():
            for level in range(levels + 1):
                at = node_at(level)
                count = max(nights >> (level + 1), 1)
                cols = b_ref[...].T
                for m in range(count):
                    node = at(2 * m)
                    vb_ref[node : node + 1] = apply(diag[node], cols[:, node : node + 1])
                if level == levels:
                    break
                cols = vb_ref[...].T
                for m in range(count):
                    node = at(2 * m)
                    column = cols[:, node : node + 1]
                    if m:
                        left = at(2 * m - 1)
                        b_ref[left : left + 1] = b_ref[left : left + 1] + apply(el(level, m), column)
                    right = at(2 * m + 1)
                    b_ref[right : right + 1] = b_ref[right : right + 1] + apply(er_t(level, m), column)
            for level in range(levels - 1, -1, -1):
                at = node_at(level)
                cols = vb_ref[...].T
                for m in range(nights >> (level + 1)):
                    node, right = at(2 * m), at(2 * m + 1)
                    value = vb_ref[node : node + 1] + apply(q_ref[q_slot(level, m), width:], cols[:, right : right + 1])
                    if m:
                        left = at(2 * m - 1)
                        value = value + apply(q_ref[q_slot(level, m), :width], cols[:, left : left + 1])
                    vb_ref[node : node + 1] = value

        start = pull[...] * scale[...]
        b_ref[...] = start
        vb_ref[...] = jnp.zeros_like(vb_ref)
        backsolve()
        guess = vb_ref[...]
        cols = guess.T
        for t in range(nights):
            r_ref[t : t + 1] = apply(saved[t], cols[:, t : t + 1])
        ahead = product(guess, cross_t[...])
        behind = product(guess, cross[...])
        zero = jnp.zeros((1, width), f32)
        rest = start - r_ref[...]
        rest = rest + jnp.concatenate([zero, ahead[:-1]], 0) + jnp.concatenate([behind[1:], zero], 0)
        b_ref[...] = rest
        backsolve()
        modes[...] = (guess + vb_ref[...]) * scale[...]

    def solve(info, pull, cross, cross_t, curve, gscale, scale):
        vm = pltpu.VMEM
        count = sum(nights >> (j + 1) for j in range(levels))
        return pl.pallas_call(
            body,
            out_shape=jax.ShapeDtypeStruct((nights, width), f32),
            scratch_shapes=[
                vm((nights, width, width), f32),
                vm((nights, width, width), f32),
                vm((max(slots - nights // 2, 1) + 8, width, width), f32),
                vm((max(slots - nights // 2, 1) + 8, width, width), f32),
                vm((max(nights // 4, 1), block, 2 * block), f32),
                vm((nights, width), f32),
                vm((nights, width), f32),
                vm((nights, width), f32),
                vm((count, 2 * width, width), f32),
            ],
            compiler_params=pltpu.CompilerParams(vmem_limit_bytes=56 << 20),
        )(info, pull, cross, cross_t, curve, gscale, scale)

    return solve


def exchange(value, axis, mask):
    count = lax.axis_size(axis)
    return lax.ppermute(value, axis, [(i, i ^ mask) for i in range(count)])


def per_device(flux, observed, loadings, channel, decay, mixing, process_precision):
    nights, stars = flux.shape
    block = loadings.shape[1]
    width = mixing.shape[0]
    groups = width // block
    seen = observed.astype(bf16)
    member = channel[None, :] == jnp.arange(groups)[:, None]
    picks = (seen[:, None, :] * member[None].astype(bf16)).reshape(nights * groups, stars)
    flat = loadings.T
    masked = (picks[:, None, :] * flat[None]).reshape(nights * groups * block, stars)
    grams = jnp.dot(masked, loadings, preferred_element_type=f32).reshape(nights, width, block)
    pulls = jnp.dot((flux[:, None, :] * picks.reshape(nights, groups, stars)).reshape(nights * groups, stars), loadings, preferred_element_type=f32)
    pulls = pulls.reshape(nights, width)
    tile = (nights, groups, block, block)
    row = lax.broadcasted_iota(jnp.int32, tile[1:], 1)
    col = lax.broadcasted_iota(jnp.int32, tile[1:], 2)
    grams = grams.reshape(tile)
    mixed = jnp.where(col >= row, grams[0], grams[1])
    spine = jnp.sum(jnp.where(col == row, grams[1], 0.0), 2)
    packed = jnp.concatenate([part.reshape(-1, 128) for part in (mixed, pulls, spine)], 0)
    mask = 1
    while mask < lax.axis_size("star"):
        packed = packed + exchange(packed, "star", mask)
        mask *= 2
    rank = lax.axis_index("night")
    mask = 1
    whole = packed[None]
    while mask < lax.axis_size("night"):
        other = exchange(whole, "night", mask)
        low = (rank & mask) == 0
        whole = jnp.where(low, jnp.concatenate([whole, other], 0), jnp.concatenate([other, whole], 0))
        mask *= 2
    total = lax.axis_size("night") * nights
    ends = [width * block // 128, (width * block + nights * width) // 128]
    mixed = whole[:, : ends[0]].reshape(-1, groups, block, block)
    flipped = jnp.swapaxes(mixed, 2, 3)
    spine = whole[:, ends[1] :].reshape(-1, groups, block, 1)
    even = jnp.where(col >= row, mixed, flipped)
    odd = jnp.where(col < row, mixed, jnp.where(col == row, spine, flipped))
    info = jnp.stack([even, odd], 1).reshape(total, width, block)
    pull = whole[:, ends[0] : ends[1]].reshape(total, width)

    root = jnp.sqrt(process_precision)
    down = 1.0 / root
    transition = jnp.diag(decay) + mixing
    cross = root[:, None] * transition * down[None, :]
    cross_t = cross.T
    curve = product(cross_t, cross)
    gscale = (down.reshape(groups, block, 1) * down.reshape(groups, 1, block)).reshape(width, block)
    solve = make_solver(total, width, block)
    all_modes = solve(info, pull, cross, cross_t, curve, gscale, down[None, :])
    modes = lax.dynamic_slice(all_modes, (rank * nights, 0), (nights, width))

    parts = []
    rest = modes.reshape(nights * groups, block)
    for _ in range(3):
        piece = lax.reduce_precision(rest, 8, 7)
        parts.append(piece.astype(bf16))
        rest = rest - piece
    fits = jnp.dot(jnp.concatenate(parts, 0), flat, preferred_element_type=f32).reshape(3, nights, groups, stars)
    fits = fits[0] + (fits[1] + fits[2])
    trend = jnp.zeros((nights, stars), f32)
    for group in range(groups):
        trend = jnp.where(member[group][None], fits[:, group], trend)
    return (modes, flux.astype(f32) - trend)


def solution(mesh):
    return jax.shard_map(
        per_device,
        mesh=mesh,
        in_specs=(P("night", "star"), P("night", "star"), P("star", None), P("star"), P(), P(), P()),
        out_specs=(P("night", None), P("night", "star")),
        check_vma=False,
    )
```
